128 devices in a mesh: tile: 16 (over z, x), seq: 8 (over y, core).
Axes of the slice: x: 4, y: 4, z: 4, core: 2. Of those that a mesh axis runs over, the one named last changes fastest.
Arguments:
- pixels: bfloat16 [8192, 128, 384], P(('tile', 'seq')), may hold values from -6 to 6
- encoder_ids: int32 [8192, 1], P(('tile', 'seq')), may hold values from 0 to 15; in each aligned block of 64 rows (0 to 63, 64 to 127, ...) at most 8 rows name the same one
- stem_weight: bfloat16 [4, 4, 3, 64], replicated, may hold values from -1.25 to 1.25
- conv_weight: bfloat16 [3, 3, 64, 128], replicated, may hold values from -0.375 to 0.375
- point_weight: bfloat16 [128, 256], replicated, may hold values from -0.75 to 0.75
- proj_weight: bfloat16 [256, 768], replicated, may hold values from -0.5 to 0.5
- qkv_weight: bfloat16 [768, 2304], replicated, may hold values from -2 to 2
- out_weight: bfloat16 [768, 768], replicated, may hold values from -0.4375 to 0.4375
Outputs:
- slide_out: bfloat16 [16, 1024, 768], P('tile', 'seq')
The draws below stay inside these ranges and needn't reach their ends.
Inputs may be any that keep to these rules, and one draw needn't show every extreme that they name: `encoder_ids`: among the 64 tiles of one reader device at most 8 name the same encoder, and in some devices one encoder is named exactly 8 times.
All inputs are finite; a program needn't handle non-finite values.
Results may differ from the reference program's by a relative error of at most 0.02.
Values may be sent and summed in bfloat16 or wider, within the bound.
A program may use at most 128 MiB of HBM per device.

```python
import math
import jax
import jax.numpy as jnp
import numpy as np
from jax import lax

PIX = 128
C1 = 64
C2 = 128
C3 = 256
D = 768
ATTENTION_HEADS = 12
HEAD_SIZE = 64
TOK_DEV = 64
TILES = 8192
CAP = 8
SEG = 128
LENGTH = 1024
N_TILE = 16
N_SEQ = 8


def draw_qkv_weight(key, part):
    normal_part = jnp.clip(jax.random.normal(key, (D, 3 * D), jnp.float32), -4.0, 4.0)
    return jnp.clip(normal_part * D ** (-0.5), -1.98, 1.98).astype(jnp.bfloat16)


def level_of(key, shape, pieces, low, largest):
    factor_of, own = 1.0, jax.random.fold_in(key, 6)
    for dim, blocks in pieces:
        draws = jnp.exp(jax.random.uniform(jax.random.fold_in(own, dim), (blocks,), jnp.float32, low / len(pieces), largest / len(pieces)))
        factor_of = factor_of * jnp.repeat(draws, shape[dim] // blocks).reshape([-1 if axis == dim else 1 for axis in range(len(shape))])
    return factor_of


def shared_out(stream_key, own, number, rows, amount, top, most, slope):
    ranking = jax.random.permutation(stream_key, amount)
    crowded, usual = portions_of(amount, rows * top, most, slope, True), portions_of(amount, rows * top, most, slope, False)
    places = jnp.arange(amount)

    def named(lengths, offset_by):
        used = int((lengths > 0).sum())
        fixed = max(1, used // 4)
        moved = fixed + (places - fixed + offset_by * (used - fixed)) % max(1, amount - fixed)
        return jnp.zeros((amount,), jnp.int32).at[ranking[jnp.where(places < fixed, places, moved)]].set(jnp.asarray(lengths, jnp.int32))

    lengths = jnp.where(number % 4 == 0, named(crowded, number // 4), named(usual, number - number // 4 - 1))
    mixed = jax.random.permutation(jax.random.fold_in(own, 3), amount)
    giver, taker = mixed[0:amount // 2 * 2:2], mixed[1:amount // 2 * 2:2]
    room = jnp.minimum(lengths[giver] - 1, most - lengths[taker]) // 2
    room = jnp.where((giver == ranking[0]) | (taker == ranking[0]) | (lengths[taker] == 0), 0, jnp.maximum(room, 0))
    moved = jax.random.randint(jax.random.fold_in(own, 4), (amount // 2,), 0, 1 << 20) % (room + 1)
    lengths = lengths.at[giver].add(-moved).at[taker].add(moved)
    items = jnp.searchsorted(jnp.cumsum(lengths), jnp.arange(rows * top), side="right").astype(jnp.int32)
    grid = items.reshape(top, rows).T
    grid = grid[jax.random.permutation(jax.random.fold_in(own, 1), rows)]
    offset_by = jax.random.randint(jax.random.fold_in(own, 2), (rows, 1), 0, top)
    return jnp.take_along_axis(grid, (jnp.arange(top)[None, :] + offset_by) % top, axis=1)


def portions_of(amount, total, reach, skew, full):
    portions = [(1 << 20) // math.isqrt(rank ** skew) + 1 for rank in range(1, amount + 1)]
    largest = reach if full else min(reach, max(-(-total // amount), total * portions[0] // sum(portions)))
    least = 1 if total - largest >= amount - 1 else 0
    given, spare = [largest] + [least] * (amount - 1), total - largest - least * (amount - 1)
    while spare > 0:
        movable = [i for i in range(1, amount) if given[i] < largest] or [i for i in range(1, amount) if given[i] < reach]
        mass, budget = sum([portions[i] for i in movable]), spare
        for i in movable:
            addition = min(reach - given[i], max(1, budget * portions[i] // mass), spare)
            given[i] = given[i] + addition
            spare = spare - addition
    return np.array(given)


def normal_values(stream_key, shape, deviation, bound, shards=(), held_as=jnp.bfloat16):
    entries = deviation * jax.random.normal(stream_key, shape, jnp.float32)
    if shards:
        entries = entries * level_of(stream_key, shape, shards, -0.22, 0.18)
    return jnp.clip(entries, -bound, bound).astype(held_as)


def setup_inputs(seed: int = 0) -> dict:
    arg_keys = jax.random.split(jax.random.key(seed), 9)
    pixels = normal_values(arg_keys[0], (TILES, PIX, PIX * 3), 1.0, 6.0, ((0, 128),))
    encoder_ids_keys = jax.random.split(jax.random.fold_in(arg_keys[1], 1), TILES // TOK_DEV)
    encoder_ids_turns = jax.random.permutation(jax.random.fold_in(arg_keys[1], 3), TILES // TOK_DEV)
    encoder_ids = jax.vmap(lambda own, number: shared_out(jax.random.fold_in(arg_keys[1], 2), own, number, TOK_DEV, N_TILE, 1, CAP, 2))(encoder_ids_keys, encoder_ids_turns).reshape((TILES, 1))
    stem_weight = normal_values(arg_keys[2], (4, 4, 3, C1), 24 ** -0.5, 1.25)
    conv_weight = normal_values(arg_keys[3], (3, 3, C1, C2), (9 * C1 // 2) ** -0.5, 0.375)
    point_weight = normal_values(arg_keys[4], (C2, C3), (C2 // 2) ** -0.5, 0.75)
    proj_weight = normal_values(arg_keys[5], (C3, D), (C3 // 2) ** -0.5, 0.5)
    qkv_weight = draw_qkv_weight(jax.random.fold_in(arg_keys[8], 71), 0)
    out_weight = normal_values(arg_keys[7], (D, D), (D // 4) ** -0.5, 0.4375)
    return {"pixels": pixels, "encoder_ids": encoder_ids, "stem_weight": stem_weight, "conv_weight": conv_weight, "point_weight": point_weight, "proj_weight": proj_weight, "qkv_weight": qkv_weight, "out_weight": out_weight}


def conv_stack(tiles, stem_weight, conv_weight, point_weight, proj_weight):
    tile_count = tiles.shape[0]
    tile_side = tiles.shape[1]
    picture = tiles.reshape(tile_count, tile_side, tile_side, 3)
    layout_spec = ('NHWC', 'HWIO', 'NHWC')
    stem_out = lax.conv_general_dilated(picture, stem_weight, (4, 4), 'VALID', dimension_numbers=layout_spec, preferred_element_type=jnp.float32)
    stem_out = jax.nn.relu(stem_out).astype(jnp.bfloat16)
    middle = lax.conv_general_dilated(stem_out, conv_weight, (2, 2), ((1, 1), (1, 1)), dimension_numbers=layout_spec, preferred_element_type=jnp.float32)
    middle = jax.nn.relu(middle).astype(jnp.bfloat16)
    point_out = jnp.einsum('nhwc,cd->nhwd', middle[:, ::2, ::2, :], point_weight, preferred_element_type=jnp.float32)
    pooled = lax.optimization_barrier(jnp.mean(jax.nn.relu(point_out), axis=(1, 2))).astype(jnp.bfloat16)
    return jnp.dot(pooled, proj_weight, preferred_element_type=jnp.float32).astype(jnp.bfloat16)

def slide_layer(rows, live, qkv_weight, out_weight):
    wide = rows.astype(jnp.float32)
    power = lax.optimization_barrier(jnp.mean(wide * wide, axis=-1, keepdims=True))
    normed = (wide * lax.rsqrt(power + 1e-06)).astype(jnp.bfloat16)
    packed = jnp.dot(normed, qkv_weight, preferred_element_type=jnp.float32)
    query_rows = packed[:, :D].astype(jnp.bfloat16).astype(jnp.float32).reshape(LENGTH, ATTENTION_HEADS, HEAD_SIZE)
    key_rows = packed[:, D:2 * D].astype(jnp.bfloat16).astype(jnp.float32).reshape(LENGTH, ATTENTION_HEADS, HEAD_SIZE)
    value_rows = packed[:, 2 * D:].astype(jnp.bfloat16).astype(jnp.float32).reshape(LENGTH, ATTENTION_HEADS, HEAD_SIZE)
    scores = jnp.einsum('phd,qhd->hpq', query_rows, key_rows) / jnp.sqrt(jnp.float32(HEAD_SIZE))
    places = jnp.arange(LENGTH)
    alive = live > 0.5
    local = (places[:, None] // SEG == places[None, :] // SEG) & (alive[None, :] | (places[:, None] == places[None, :]))
    offsets = jnp.arange(ATTENTION_HEADS) % N_SEQ
    picked = (places % N_SEQ)[None, :] == offsets[:, None]
    dilated = picked[:, :, None] & picked[:, None, :] & alive[None, None, :]
    counts = local.astype(jnp.float32)[None] + dilated.astype(jnp.float32)
    masked = jnp.where(counts > 0, scores, jnp.float32(-1e+30))
    top = lax.optimization_barrier(jnp.max(masked, axis=-1, keepdims=True))
    weights = jnp.exp(masked - top) * counts
    total = lax.optimization_barrier(jnp.sum(weights, axis=-1, keepdims=True))
    context = jnp.einsum('hpq,qhd->hpd', weights, value_rows) / total
    context = jnp.transpose(context, (1, 0, 2)).reshape(LENGTH, D).astype(jnp.bfloat16)
    result = jnp.dot(context, out_weight, preferred_element_type=jnp.float32) * live[:, None]
    return result.astype(jnp.bfloat16)

def reference(pixels, encoder_ids, stem_weight, conv_weight, point_weight, proj_weight, qkv_weight, out_weight):
    n_devices = N_TILE * N_SEQ
    blocks = pixels.reshape(n_devices, TOK_DEV, PIX, PIX * 3)
    embeds = lax.map(lambda block: conv_stack(block, stem_weight, conv_weight, point_weight, proj_weight), blocks)
    targets = encoder_ids.reshape(n_devices, TOK_DEV).astype(jnp.int32)
    order = jnp.arange(TOK_DEV, dtype=jnp.int32)
    same = (targets[:, :, None] == targets[:, None, :]) & (order[None, None, :] < order[None, :, None])
    ranks = lax.optimization_barrier(jnp.sum(same.astype(jnp.int32), axis=2))
    device = jnp.arange(n_devices, dtype=jnp.int32)[:, None]
    position = device % N_SEQ * SEG + device // N_SEQ * CAP + ranks
    slides = jnp.zeros((N_TILE, LENGTH, D), jnp.bfloat16).at[targets, position].set(embeds)
    live = jnp.zeros((N_TILE, LENGTH), jnp.float32).at[targets, position].set(1.0)
    return lax.map(lambda pair: slide_layer(pair[0], pair[1], qkv_weight, out_weight), (slides, live))
```

```python
import functools
import jax
import jax.numpy as jnp
from jax import lax
from jax.sharding import PartitionSpec as P
from jax.experimental import pallas as pl
from jax.experimental.pallas import tpu as pltpu

D = 768
C1, C2, C3 = 64, 128, 256
GROUP = 16
LINE = D + 128
F32, BF16 = jnp.float32, jnp.bfloat16

BLOCKS = (
    ((0, 0, 1), (1, 0, 2), (3, 1, 0), (4, 1, 1)),
    ((5, 0, 2), (7, 1, 0), (8, 1, 1), (9, 1, 2)),
    ((11, 0, 0), (12, 0, 1), (13, 0, 2), (15, 1, 0)),
)


def iota(shape, dim):
    return lax.broadcasted_iota(jnp.int32, shape, dim)


def dot(a, b):
    return jnp.dot(a, b, preferred_element_type=F32)


def stem_spread(stem_ref, flat_ref, base):
    taps = iota((256, 64), 1)
    rows = iota((256, 64), 0)
    lane = (rows & 63) + base
    lane = lane - 12 * jnp.floor((lane.astype(F32) + 0.5) * (1.0 / 12.0)).astype(jnp.int32)
    colour, column = (taps & 15) >> 2, taps & 3
    hit = ((rows >> 6) == (taps >> 4)) & (colour < 3) & (lane == 3 * column + colour)
    chosen = jnp.where(hit, 1.0, 0.0).astype(BF16)
    tiled = jnp.where((iota((64, 256), 1) & 63) == iota((64, 256), 0), 1.0, 0.0).astype(BF16)
    wide = dot(flat_ref[...].astype(BF16), tiled).astype(BF16)
    return dot(chosen, wide)


def stem_block(spread, base, block):
    lane = (iota((256, 256), 0) & 63) + base
    quarter = iota((256, 256), 1) >> 6
    first = jnp.zeros((256, 256), jnp.int32)
    for q, (column, _, _) in enumerate(block):
        first = jnp.where(quarter == q, 12 * column, first)
    return jnp.where((lane >= first) & (lane < first + 12), spread, 0.0).astype(BF16)


def encode_kernel(steps, pix_ref, ids_ref, stem_ref, conv_ref, point_ref, proj_ref, out_ref,
                  flat, stem_w, conv_w, picked, packed, hidden, middle, pooled):
    step = pl.program_id(0)
    n_tiles = pix_ref.shape[0] // 128
    n_blocks = n_tiles // 2
    n_rows = n_tiles * 8

    @pl.when(step == 0)
    def _():
        flat[...] = jnp.zeros_like(flat)
        for a in range(4):
            for c in range(3):
                flat[a * 16 + c * 4:a * 16 + c * 4 + 4, :] = stem_ref[a, c].astype(F32)
        for base, uses in ((0, ((0, 0), (1, 1))), (64, ((2, 1),)), (128, ((3, 2),))):
            spread = stem_spread(stem_ref, flat, base)
            for slot, block in uses:
                stem_w[slot] = stem_block(spread, base, BLOCKS[block])
        conv_w[...] = jnp.zeros_like(conv_w)
        for n, block in enumerate(BLOCKS):
            for d in range(3):
                for q, (_, side, tap) in enumerate(block):
                    row = d * 256 + q * 64
                    conv_w[n, row:row + 64, side * 128:side * 128 + 128] = conv_ref[d, tap]
        row, col = iota((192, 256), 0), iota((192, 256), 1)
        tap_row, g = row >> 4, row & 15
        a, d = tap_row & 3, tap_row >> 2
        row_of = 16 * g + 4 * (d - 1) + a
        good = (row_of == col) & ((d > 0) | ((g & 7) > 0))
        picked[...] = jnp.where(good, 1.0, 0.0).astype(BF16)

    for b in range(n_blocks):
        rows = dot(picked[...], pix_ref[b * 256:b * 256 + 256, :]).astype(BF16)
        for d in range(3):
            for pair in range(2):
                first = (d * 4 + pair * 2) * 16
                p0, p1 = rows[first:first + 16], rows[first + 16:first + 32]
                for c in range(3):
                    lo = c * 128
                    for half in range(2):
                        unit = 2 * c + half
                        at = lo + half * 64
                        h, u = unit // 3, unit % 3
                        packed[u, (h * 3 + d) * n_rows + b * 16:(h * 3 + d) * n_rows + b * 16 + 16,
                               pair * 128:pair * 128 + 128] = jnp.concatenate(
                                   [p0[:, at:at + 64], p1[:, at:at + 64]], axis=1)

    for n, terms in enumerate((((0, 0),), ((0, 1), (1, 2)), ((2, 3),))):
        total = dot(packed[terms[0][0]], stem_w[terms[0][1]])
        for u, w in terms[1:]:
            total = total + dot(packed[u], stem_w[w])
        total = jnp.maximum(total, 0.0).astype(BF16)
        for h in range(2):
            for d in range(3):
                hidden[n, h * n_rows:(h + 1) * n_rows, d * 256:(d + 1) * 256] = (
                    total[(h * 3 + d) * n_rows:(h * 3 + d + 1) * n_rows])
    left = dot(hidden[0], conv_w[0])
    mid = dot(hidden[1], conv_w[1])
    right = dot(hidden[2], conv_w[2])
    for h in range(2):
        rows = slice(h * n_rows, (h + 1) * n_rows)
        first = left[rows, :128]
        if h == 1:
            first = first + right[:n_rows, 128:]
        cols = (first, left[rows, 128:] + mid[rows, :128], mid[rows, 128:], right[rows, :128])
        for j, col in enumerate(cols):
            at = (h * 4 + j) * n_rows
            middle[at:at + n_rows, :] = jnp.maximum(col, 0.0).astype(BF16)
    point = jnp.maximum(dot(middle[...], point_ref[...]), 0.0)
    summed = point[:n_rows]
    for j in range(1, 8):
        summed = summed + point[j * n_rows:(j + 1) * n_rows]
    mean = jnp.sum(summed.reshape(n_tiles, 8, C3), axis=1) * (1.0 / 64.0)
    pooled[pl.ds(pl.multiple_of(step * n_tiles, n_tiles), n_tiles), :] = mean.astype(BF16)

    @pl.when(step == steps - 1)
    def _():
        embed = dot(pooled[...], proj_ref[...]).astype(BF16)
        n = embed.shape[0]
        across = jnp.broadcast_to(ids_ref[...], (n, n))
        own = iota((n, n), 0) == iota((n, n), 1)
        down = jnp.sum(jnp.where(own, across, 0), axis=1, keepdims=True)
        same = (down == across) & (iota((n, n), 0) < iota((n, n), 1))
        rank = jnp.sum(jnp.where(same, 1, 0), axis=0, keepdims=True)
        slot = ids_ref[...] * 8 + rank
        n_slots = out_ref.shape[0] * 8
        placed = jnp.where(iota((n_slots, n), 0) == slot, 1.0, 0.0)
        live = jnp.sum(placed, axis=1, keepdims=True)
        routed = dot(placed.astype(BF16), embed)
        out_ref[:, :, :D] = routed.reshape(n_slots // 8, 8, D).astype(BF16)
        out_ref[:, :, D:] = jnp.broadcast_to(live, (n_slots, 128)).reshape(n_slots // 8, 8, 128).astype(BF16)


def encode(pixels, encoder_ids, stem_weight, conv_weight, point_weight, proj_weight, n_tile, steps=4):
    n = pixels.shape[0]
    flat_pixels = pixels.reshape(n * 128, 384)
    rows = n * 128 // steps
    n_rows = rows // 16
    stem_t = jnp.transpose(stem_weight, (0, 2, 1, 3))
    whole = lambda shape: pl.BlockSpec(shape, lambda i: (0,) * len(shape))
    return pl.pallas_call(
        functools.partial(encode_kernel, steps),
        grid=(steps,),
        in_specs=[
            pl.BlockSpec((rows, 384), lambda i: (i, 0)),
            whole((1, n)),
            whole(stem_t.shape),
            whole(conv_weight.shape),
            whole(point_weight.shape),
            whole(proj_weight.shape),
        ],
        out_specs=whole((n_tile, 8, LINE)),
        out_shape=jax.ShapeDtypeStruct((n_tile, 8, LINE), BF16),
        scratch_shapes=[
            pltpu.VMEM((64, 64), F32),
            pltpu.VMEM((4, 256, 256), BF16),
            pltpu.VMEM((3, 768, 256), BF16),
            pltpu.VMEM((192, 256), BF16),
            pltpu.VMEM((3, 6 * n_rows, 256), BF16),
            pltpu.VMEM((3, 2 * n_rows, 768), BF16),
            pltpu.VMEM((8 * n_rows, 128), BF16),
            pltpu.VMEM((n, C3), BF16),
        ],
        name="encode_tiles",
    )(flat_pixels, encoder_ids.reshape(1, n), stem_t, conv_weight, point_weight, proj_weight)

ATTENTION_HEADS = 12
HEAD_SIZE = 64


def slide_layer(rows, live, qkv_weight, out_weight):
    sequence_count = lax.axis_size("seq")
    seg_len = rows.shape[0]
    dilation_groups = seg_len // sequence_count
    wide = rows.astype(jnp.float32)
    power = jnp.mean(wide * wide, axis=-1, keepdims=True)
    normed = (wide * lax.rsqrt(power + 1e-06)).astype(jnp.bfloat16)
    packed = jnp.dot(normed, qkv_weight, preferred_element_type=jnp.float32)
    query_rows = (
        packed[:, :D]
        .astype(jnp.bfloat16)
        .astype(jnp.float32)
        .reshape(seg_len, ATTENTION_HEADS, HEAD_SIZE)
    )
    keys_bf = packed[:, D : 2 * D].astype(jnp.bfloat16)
    values_bf = packed[:, 2 * D :].astype(jnp.bfloat16)
    key_rows = keys_bf.astype(jnp.float32).reshape(seg_len, ATTENTION_HEADS, HEAD_SIZE)
    value_rows = values_bf.astype(jnp.float32).reshape(seg_len, ATTENTION_HEADS, HEAD_SIZE)
    score_scale = 1.0 / jnp.sqrt(jnp.float32(HEAD_SIZE))
    scores = jnp.einsum("phd,qhd->hpq", query_rows, key_rows) * score_scale
    places = jnp.arange(seg_len)
    alive = live > 0.5
    local = alive[None, :] | (places[:, None] == places[None, :])
    masked = jnp.where(local[None], scores, jnp.float32(-1e30))
    top_local = jnp.max(masked, axis=-1)
    weights = jnp.exp(masked - top_local[:, :, None]) * local[None].astype(jnp.float32)
    den_local = jnp.sum(weights, axis=-1)
    local_accumulator = jnp.einsum("hpq,qhd->hpd", weights, value_rows)
    offsets = jnp.arange(ATTENTION_HEADS) % sequence_count
    dilation_selector = (jnp.arange(sequence_count)[:, None] == offsets[None, :]).astype(
        jnp.float32
    )
    selected_query = jnp.einsum(
        "bnpo,np->pbo",
        query_rows.reshape(dilation_groups, sequence_count, ATTENTION_HEADS, HEAD_SIZE),
        dilation_selector,
    )
    selected_keys = jnp.einsum(
        "bnpo,np->pbo",
        key_rows.reshape(dilation_groups, sequence_count, ATTENTION_HEADS, HEAD_SIZE),
        dilation_selector,
    ).astype(jnp.bfloat16)
    values_sel = jnp.einsum(
        "bnpo,np->pbo",
        value_rows.reshape(dilation_groups, sequence_count, ATTENTION_HEADS, HEAD_SIZE),
        dilation_selector,
    ).astype(jnp.bfloat16)
    live_sel = jnp.einsum(
        "mr,rh->hm", live.reshape(dilation_groups, sequence_count), dilation_selector
    ).astype(jnp.bfloat16)
    start_top = jnp.einsum(
        "hmr,rh->hm",
        top_local.reshape(ATTENTION_HEADS, dilation_groups, sequence_count),
        dilation_selector,
    )
    start_den = jnp.einsum(
        "hmr,rh->hm",
        den_local.reshape(ATTENTION_HEADS, dilation_groups, sequence_count),
        dilation_selector,
    )
    initial_accumulator = jnp.einsum(
        "bstc,tb->bsc",
        local_accumulator.reshape(ATTENTION_HEADS, dilation_groups, sequence_count, HEAD_SIZE),
        dilation_selector,
    )
    segment_keys = lax.all_gather(selected_keys, "seq", axis=1, tiled=True)
    segment_values = lax.all_gather(values_sel, "seq", axis=1, tiled=True)
    piece_live = lax.all_gather(live_sel, "seq", axis=1, tiled=True)
    usable = piece_live.astype(jnp.float32) > 0.5
    partial_scores = (
        jnp.einsum("psi,pei->pse", selected_query, segment_keys.astype(jnp.float32)) * score_scale
    )
    part_masked = jnp.where(usable[:, None, :], partial_scores, jnp.float32(-1e30))
    new_top = jnp.maximum(start_top, jnp.max(part_masked, axis=-1))
    rescale = jnp.exp(start_top - new_top)
    partial_weights = jnp.exp(part_masked - new_top[:, :, None]) * usable[:, None, :].astype(
        jnp.float32
    )
    new_den = start_den * rescale + jnp.sum(partial_weights, axis=-1)
    new_acc = initial_accumulator * rescale[:, :, None] + jnp.einsum(
        "zfj,zjg->zfg", partial_weights, segment_values.astype(jnp.float32)
    )
    context_sel = new_acc / new_den[:, :, None]
    context_local = (local_accumulator / den_local[:, :, None]).reshape(
        ATTENTION_HEADS, dilation_groups, sequence_count, HEAD_SIZE
    )
    choose = jnp.transpose(dilation_selector, (1, 0))[:, None, :, None]
    context = context_local * (1.0 - choose) + context_sel[:, :, None, :] * choose
    context = (
        jnp.transpose(context.reshape(ATTENTION_HEADS, seg_len, HEAD_SIZE), (1, 0, 2))
        .reshape(seg_len, D)
        .astype(jnp.bfloat16)
    )
    result = jnp.dot(context, out_weight, preferred_element_type=jnp.float32) * live[:, None]
    return result.astype(jnp.bfloat16)


def body(
    pixels, encoder_ids, stem_weight, conv_weight, point_weight, proj_weight, qkv_weight, out_weight
):
    n_tile = lax.axis_size("tile")
    sent = encode(pixels, encoder_ids, stem_weight, conv_weight, point_weight, proj_weight, n_tile)
    got = lax.all_to_all(sent, "tile", split_axis=0, concat_axis=0, tiled=True)
    got = got.reshape(-1, LINE)
    return slide_layer(got[:, :D], got[:, D].astype(F32), qkv_weight, out_weight)[None]


def solution(mesh):
    return jax.shard_map(
        body,
        mesh=mesh,
        in_specs=(
            P(("tile", "seq"), None, None),
            P(("tile", "seq"), None),
            P(),
            P(),
            P(),
            P(),
            P(),
            P(),
        ),
        out_specs=P("tile", "seq", None),
        check_vma=False,
    )
```

```python
import functools
import jax
import jax.numpy as jnp
from jax import lax
from jax.sharding import PartitionSpec as P
from jax.experimental import pallas as pl
from jax.experimental.pallas import tpu as pltpu

D = 768
C1, C2, C3 = 64, 128, 256
GROUP = 16
LINE = D + 128
HEAD_SIZE = 64
F32, BF16 = jnp.float32, jnp.bfloat16
MESH = pl.DeviceIdType.MESH

BLOCKS = (
    ((0, 0, 1), (1, 0, 2), (3, 1, 0), (4, 1, 1)),
    ((5, 0, 2), (7, 1, 0), (8, 1, 1), (9, 1, 2)),
    ((11, 0, 0), (12, 0, 1), (13, 0, 2), (15, 1, 0)),
)


def iota(shape, dim):
    return lax.broadcasted_iota(jnp.int32, shape, dim)


def dot(a, b):
    return jnp.dot(a, b, preferred_element_type=F32)


def stem_spread(stem_ref, flat_ref, base):
    taps = iota((256, 64), 1)
    rows = iota((256, 64), 0)
    lane = (rows & 63) + base
    lane = lane - 12 * jnp.floor((lane.astype(F32) + 0.5) * (1.0 / 12.0)).astype(jnp.int32)
    colour, column = (taps & 15) >> 2, taps & 3
    hit = ((rows >> 6) == (taps >> 4)) & (colour < 3) & (lane == 3 * column + colour)
    chosen = jnp.where(hit, 1.0, 0.0).astype(BF16)
    tiled = jnp.where((iota((64, 256), 1) & 63) == iota((64, 256), 0), 1.0, 0.0).astype(BF16)
    wide = dot(flat_ref[...].astype(BF16), tiled).astype(BF16)
    return dot(chosen, wide)


def stem_block(spread, base, block):
    lane = (iota((256, 256), 0) & 63) + base
    quarter = iota((256, 256), 1) >> 6
    first = jnp.zeros((256, 256), jnp.int32)
    for q, (column, _, _) in enumerate(block):
        first = jnp.where(quarter == q, 12 * column, first)
    return jnp.where((lane >= first) & (lane < first + 12), spread, 0.0).astype(BF16)


def encode_kernel(steps, pix_ref, ids_ref, stem_ref, conv_ref, point_ref, proj_ref, out_ref,
                  flat, stem_w, conv_w, picked, packed, hidden, middle, pooled):
    step = pl.program_id(0)
    n_tiles = pix_ref.shape[0] // 128
    n_blocks = n_tiles // 2
    n_rows = n_tiles * 8

    @pl.when(step == 0)
    def _():
        flat[...] = jnp.zeros_like(flat)
        for a in range(4):
            for c in range(3):
                flat[a * 16 + c * 4:a * 16 + c * 4 + 4, :] = stem_ref[a, c].astype(F32)
        for base, uses in ((0, ((0, 0), (1, 1))), (64, ((2, 1),)), (128, ((3, 2),))):
            spread = stem_spread(stem_ref, flat, base)
            for slot, block in uses:
                stem_w[slot] = stem_block(spread, base, BLOCKS[block])
        conv_w[...] = jnp.zeros_like(conv_w)
        for n, block in enumerate(BLOCKS):
            for d in range(3):
                for q, (_, side, tap) in enumerate(block):
                    row = d * 256 + q * 64
                    conv_w[n, row:row + 64, side * 128:side * 128 + 128] = conv_ref[d, tap]
        row, col = iota((192, 256), 0), iota((192, 256), 1)
        tap_row, g = row >> 4, row & 15
        a, d = tap_row & 3, tap_row >> 2
        row_of = 16 * g + 4 * (d - 1) + a
        good = (row_of == col) & ((d > 0) | ((g & 7) > 0))
        picked[...] = jnp.where(good, 1.0, 0.0).astype(BF16)

    for b in range(n_blocks):
        rows = dot(picked[...], pix_ref[b * 256:b * 256 + 256, :]).astype(BF16)
        for d in range(3):
            for pair in range(2):
                first = (d * 4 + pair * 2) * 16
                p0, p1 = rows[first:first + 16], rows[first + 16:first + 32]
                for c in range(3):
                    lo = c * 128
                    for half in range(2):
                        unit = 2 * c + half
                        at = lo + half * 64
                        h, u = unit // 3, unit % 3
                        packed[u, (h * 3 + d) * n_rows + b * 16:(h * 3 + d) * n_rows + b * 16 + 16,
                               pair * 128:pair * 128 + 128] = jnp.concatenate(
                                   [p0[:, at:at + 64], p1[:, at:at + 64]], axis=1)

    for n, terms in enumerate((((0, 0),), ((0, 1), (1, 2)), ((2, 3),))):
        total = dot(packed[terms[0][0]], stem_w[terms[0][1]])
        for u, w in terms[1:]:
            total = total + dot(packed[u], stem_w[w])
        total = jnp.maximum(total, 0.0).astype(BF16)
        for h in range(2):
            for d in range(3):
                hidden[n, h * n_rows:(h + 1) * n_rows, d * 256:(d + 1) * 256] = (
                    total[(h * 3 + d) * n_rows:(h * 3 + d + 1) * n_rows])
    left = dot(hidden[0], conv_w[0])
    mid = dot(hidden[1], conv_w[1])
    right = dot(hidden[2], conv_w[2])
    for h in range(2):
        rows = slice(h * n_rows, (h + 1) * n_rows)
        first = left[rows, :128]
        if h == 1:
            first = first + right[:n_rows, 128:]
        cols = (first, left[rows, 128:] + mid[rows, :128], mid[rows, 128:], right[rows, :128])
        for j, col in enumerate(cols):
            at = (h * 4 + j) * n_rows
            middle[at:at + n_rows, :] = jnp.maximum(col, 0.0).astype(BF16)
    point = jnp.maximum(dot(middle[...], point_ref[...]), 0.0)
    summed = point[:n_rows]
    for j in range(1, 8):
        summed = summed + point[j * n_rows:(j + 1) * n_rows]
    mean = jnp.sum(summed.reshape(n_tiles, 8, C3), axis=1) * (1.0 / 64.0)
    pooled[pl.ds(pl.multiple_of(step * n_tiles, n_tiles), n_tiles), :] = mean.astype(BF16)

    @pl.when(step == steps - 1)
    def _():
        embed = dot(pooled[...], proj_ref[...]).astype(BF16)
        n = embed.shape[0]
        across = jnp.broadcast_to(ids_ref[...], (n, n))
        own = iota((n, n), 0) == iota((n, n), 1)
        down = jnp.sum(jnp.where(own, across, 0), axis=1, keepdims=True)
        same = (down == across) & (iota((n, n), 0) < iota((n, n), 1))
        rank = jnp.sum(jnp.where(same, 1, 0), axis=0, keepdims=True)
        slot = ids_ref[...] * 8 + rank
        n_slots = out_ref.shape[0] * 8
        placed = jnp.where(iota((n_slots, n), 0) == slot, 1.0, 0.0)
        live = jnp.sum(placed, axis=1, keepdims=True)
        routed = dot(placed.astype(BF16), embed)
        out_ref[:, :, :D] = routed.reshape(n_slots // 8, 8, D).astype(BF16)
        out_ref[:, :, D:] = jnp.broadcast_to(live, (n_slots, 128)).reshape(n_slots // 8, 8, 128).astype(BF16)


def encode(pixels, encoder_ids, stem_weight, conv_weight, point_weight, proj_weight, n_tile, steps=4):
    n = pixels.shape[0]
    flat_pixels = pixels.reshape(n * 128, 384)
    rows = n * 128 // steps
    n_rows = rows // 16
    stem_t = jnp.transpose(stem_weight, (0, 2, 1, 3))
    whole = lambda shape: pl.BlockSpec(shape, lambda i: (0,) * len(shape))
    return pl.pallas_call(
        functools.partial(encode_kernel, steps),
        grid=(steps,),
        in_specs=[
            pl.BlockSpec((rows, 384), lambda i: (i, 0)),
            whole((1, n)),
            whole(stem_t.shape),
            whole(conv_weight.shape),
            whole(point_weight.shape),
            whole(proj_weight.shape),
        ],
        out_specs=whole((n_tile, 8, LINE)),
        out_shape=jax.ShapeDtypeStruct((n_tile, 8, LINE), BF16),
        scratch_shapes=[
            pltpu.VMEM((64, 64), F32),
            pltpu.VMEM((4, 256, 256), BF16),
            pltpu.VMEM((3, 768, 256), BF16),
            pltpu.VMEM((192, 256), BF16),
            pltpu.VMEM((3, 6 * n_rows, 256), BF16),
            pltpu.VMEM((3, 2 * n_rows, 768), BF16),
            pltpu.VMEM((8 * n_rows, 128), BF16),
            pltpu.VMEM((n, C3), BF16),
        ],
        name="encode_tiles",
    )(flat_pixels, encoder_ids.reshape(1, n), stem_t, conv_weight, point_weight, proj_weight)


def spread_rows(n, minor):
    row, col = iota((n, n), 0), iota((n, n), 1)
    shift = minor.bit_length() - 1
    return jnp.where(col == (row & (minor - 1)) * (n // minor) + (row >> shift), 1.0, 0.0).astype(BF16)


def dot_t(a, b):
    return lax.dot_general(a, b, (((1,), (1,)), ((), ())), preferred_element_type=F32)


def layer_kernel(n_tile, n_seq, sent, qkv_hbm, out_hbm, o_ref, got, qkv_w, out_w, kv_send, kv_all, context,
                 weight_sem, own_sem, send_sem, recv_sem, kv_send_sem, kv_recv_sem):
    t, s = lax.axis_index("tile"), lax.axis_index("seq")
    load_qkv = pltpu.make_async_copy(qkv_hbm, qkv_w, weight_sem.at[0])
    load_out = pltpu.make_async_copy(out_hbm, out_w, weight_sem.at[1])
    load_qkv.start()
    load_out.start()
    barrier = pltpu.get_barrier_semaphore()
    for k in range(1, n_tile):
        pl.semaphore_signal(barrier, inc=1, device_id={"tile": lax.rem(t + k, n_tile)}, device_id_type=MESH)
    for k in range(1, n_seq):
        pl.semaphore_signal(barrier, inc=1, device_id={"seq": lax.rem(s + k, n_seq)}, device_id_type=MESH)
    keep = pltpu.make_async_copy(sent.at[t], got.at[t], own_sem)
    keep.start()
    pl.semaphore_wait(barrier, n_tile + n_seq - 2)
    moves = []
    for k in range(1, n_tile):
        peer = lax.rem(t + k, n_tile)
        moves.append(pltpu.make_async_remote_copy(
            src_ref=sent.at[peer], dst_ref=got.at[t], send_sem=send_sem.at[k - 1], recv_sem=recv_sem.at[k - 1],
            device_id={"tile": peer}, device_id_type=MESH))
        moves[-1].start()
    n = n_tile * 8
    low = iota((n, 128), 1) < HEAD_SIZE
    keep.wait()
    for move in moves:
        move.wait()

    natural = got[...].astype(F32).reshape(n, LINE)
    rows = dot(spread_rows(n, n_tile), natural.astype(BF16))
    live = rows[:, D:]
    rows = rows[:, :D]
    power = jnp.mean(rows * rows, axis=-1, keepdims=True)
    normed = (rows * lax.rsqrt(power + 1e-06)).astype(BF16)
    load_qkv.wait()
    pairs = D // 128
    kv = dot(normed, qkv_w[:, D:]).astype(BF16)
    low16 = low[:n_tile]

    def offsets(m):
        a = (2 * m) % n_seq
        b = (2 * m + 1) % n_seq
        return slice(a * n_tile, (a + 1) * n_tile), slice(b * n_tile, (b + 1) * n_tile)

    for m in range(2 * pairs):
        chunk = kv[:, m * 128:(m + 1) * 128]
        first, second = offsets(m % pairs)
        kv_send[m] = jnp.where(low16, chunk[first], chunk[second])
    flags = jnp.zeros((n_tile, 128), F32)
    for r in range(n_seq):
        flags = jnp.where(iota((n_tile, 128), 1) == r, live[r * n_tile:(r + 1) * n_tile], flags)
    kv_send[2 * pairs] = flags.astype(BF16)
    kv_moves = []
    for k in range(1, n_seq):
        peer = lax.rem(s + k, n_seq)
        kv_moves.append(pltpu.make_async_remote_copy(
            src_ref=kv_send, dst_ref=kv_all.at[s], send_sem=kv_send_sem.at[k - 1], recv_sem=kv_recv_sem.at[k - 1],
            device_id={"seq": peer}, device_id_type=MESH))
        kv_moves[-1].start()
    kv_all[s] = kv_send[...]

    query = (dot(normed, qkv_w[:, :D]).astype(BF16) * 0.125).astype(BF16)
    live_across = jnp.transpose(live)
    own = iota((n, n), 0) == iota((n, n), 1)
    bias = jnp.where((live_across > 0.5) | own, 0.0, -1e30)
    bias = jnp.concatenate([bias, bias], axis=0)
    none = jnp.zeros((n, 128), BF16)
    kept = []
    for m in range(pairs):
        lanes = slice(m * 128, (m + 1) * 128)
        q = query[:, lanes]
        q = jnp.concatenate([jnp.where(low, q, none), jnp.where(low, none, q)], axis=0)
        score = dot_t(q, kv[:, lanes]) + bias
        top = jnp.max(score, axis=-1, keepdims=True)
        weight = jnp.exp(score - top)
        total = jnp.sum(weight, axis=-1, keepdims=True)
        summed = dot(weight.astype(BF16), kv[:, D + m * 128:D + (m + 1) * 128])
        result = summed / total
        context[:, lanes] = jnp.where(low, result[:n], result[n:]).astype(BF16)
        first, second = offsets(m)
        second = slice(n + second.start, n + second.stop)
        kept.append([jnp.concatenate([x[first], x[second]], axis=0) for x in (q, top, total, summed)])

    for move in kv_moves:
        move.wait()
    there = kv_all[:, 2 * pairs].reshape(n, 128)
    pick = jnp.where(iota((n_tile, 128), 0) == iota((n_tile, 128), 1), 1.0, 0.0).astype(BF16)
    far_bias = jnp.where(dot_t(pick, there) > 0.5, 0.0, -1e30)
    for m in range(pairs):
        lanes = slice(m * 128, (m + 1) * 128)
        first, second = offsets(m)
        q, top, total, summed = kept[m]
        a, b = first.start // n_tile, second.start // n_tile
        far = jnp.concatenate([jnp.broadcast_to(far_bias[a:a + 1], (n_tile, 128)),
                               jnp.broadcast_to(far_bias[b:b + 1], (n_tile, 128))], axis=0)
        score = dot_t(q, kv_all[:, m].reshape(n, 128)) + far
        new_top = jnp.maximum(top, jnp.max(score, axis=-1, keepdims=True))
        weight = jnp.exp(score - new_top)
        scale = jnp.exp(top - new_top)
        total = total * scale + jnp.sum(weight, axis=-1, keepdims=True)
        summed = summed * scale + dot(weight.astype(BF16), kv_all[:, pairs + m].reshape(n, 128))
        result = (summed / total).astype(BF16)
        context[first, lanes] = jnp.where(low16, result[:n_tile], context[first, lanes])
        context[second, lanes] = jnp.where(low16, context[second, lanes], result[n_tile:])

    back = dot(spread_rows(n, n_seq), context[...]).astype(BF16)
    load_out.wait()
    final = dot(back, out_w[...])
    alive = natural[:, D:] > 0.5
    for m in range(pairs):
        lanes = slice(m * 128, (m + 1) * 128)
        o_ref[:, lanes] = jnp.where(alive, final[:, lanes], 0.0).astype(BF16)


def slide_layer(sent, qkv_weight, out_weight):
    n_tile, n_seq = lax.axis_size("tile"), lax.axis_size("seq")
    n = n_tile * 8
    anywhere = pl.BlockSpec(memory_space=pl.ANY)
    blocks = 2 * D // 128 + 1
    return pl.pallas_call(
        functools.partial(layer_kernel, n_tile, n_seq),
        in_specs=[anywhere] * 3,
        out_specs=pl.BlockSpec(memory_space=pltpu.VMEM),
        out_shape=jax.ShapeDtypeStruct((n, D), BF16),
        scratch_shapes=[
            pltpu.VMEM((n_tile, 8, LINE), BF16),
            pltpu.VMEM(qkv_weight.shape, BF16),
            pltpu.VMEM(out_weight.shape, BF16),
            pltpu.VMEM((blocks, n_tile, 128), BF16),
            pltpu.VMEM((n_seq, blocks, n_tile, 128), BF16),
            pltpu.VMEM((n, D), BF16),
            pltpu.SemaphoreType.DMA((2,)),
            pltpu.SemaphoreType.DMA,
            pltpu.SemaphoreType.DMA((n_tile - 1,)),
            pltpu.SemaphoreType.DMA((n_tile - 1,)),
            pltpu.SemaphoreType.DMA((n_seq - 1,)),
            pltpu.SemaphoreType.DMA((n_seq - 1,)),
        ],
        compiler_params=pltpu.CompilerParams(collective_id=0, has_side_effects=True),
        name="slide_layer",
    )(sent, qkv_weight, out_weight)


def body(
    pixels, encoder_ids, stem_weight, conv_weight, point_weight, proj_weight, qkv_weight, out_weight
):
    n_tile = lax.axis_size("tile")
    sent = encode(pixels, encoder_ids, stem_weight, conv_weight, point_weight, proj_weight, n_tile)
    return slide_layer(sent, qkv_weight, out_weight)[None]


def solution(mesh):
    return jax.shard_map(
        body,
        mesh=mesh,
        in_specs=(
            P(("tile", "seq"), None, None),
            P(("tile", "seq"), None),
            P(),
            P(),
            P(),
            P(),
            P(),
            P(),
        ),
        out_specs=P("tile", "seq", None),
        check_vma=False,
    )
```

```python
import functools
import jax
import jax.numpy as jnp
from jax import lax
from jax.sharding import PartitionSpec as P
from jax.experimental import pallas as pl
from jax.experimental.pallas import tpu as pltpu

D = 768
C1, C2, C3 = 64, 128, 256
GROUP = 16
LINE = D + 128
HEAD_SIZE = 64
F32, BF16 = jnp.float32, jnp.bfloat16
MESH = pl.DeviceIdType.MESH

BLOCKS = (
    ((0, 0, 1), (1, 0, 2), (3, 1, 0), (4, 1, 1)),
    ((5, 0, 2), (7, 1, 0), (8, 1, 1), (9, 1, 2)),
    ((11, 0, 0), (12, 0, 1), (13, 0, 2), (15, 1, 0)),
)


def iota(shape, dim):
    return lax.broadcasted_iota(jnp.int32, shape, dim)


def dot(a, b):
    return jnp.dot(a, b, preferred_element_type=F32)


def stem_spread(stem_ref, flat_ref, base):
    taps = iota((256, 64), 1)
    rows = iota((256, 64), 0)
    lane = (rows & 63) + base
    lane = lane - 12 * jnp.floor((lane.astype(F32) + 0.5) * (1.0 / 12.0)).astype(jnp.int32)
    colour, column = (taps & 15) >> 2, taps & 3
    hit = ((rows >> 6) == (taps >> 4)) & (colour < 3) & (lane == 3 * column + colour)
    chosen = jnp.where(hit, 1.0, 0.0).astype(BF16)
    tiled = jnp.where((iota((64, 256), 1) & 63) == iota((64, 256), 0), 1.0, 0.0).astype(BF16)
    wide = dot(flat_ref[...].astype(BF16), tiled).astype(BF16)
    return dot(chosen, wide)


def stem_block(spread, base, block):
    lane = (iota((256, 256), 0) & 63) + base
    quarter = iota((256, 256), 1) >> 6
    first = jnp.zeros((256, 256), jnp.int32)
    for q, (column, _, _) in enumerate(block):
        first = jnp.where(quarter == q, 12 * column, first)
    return jnp.where((lane >= first) & (lane < first + 12), spread, 0.0).astype(BF16)


def prepare(stem_ref, conv_ref, flat, stem_w, conv_w, picked):
    flat[...] = jnp.zeros_like(flat)
    for a in range(4):
        for c in range(3):
            flat[a * 16 + c * 4:a * 16 + c * 4 + 4, :] = stem_ref[a, c].astype(F32)
    for base, uses in ((0, ((0, 0), (1, 1))), (64, ((2, 1),)), (128, ((3, 2),))):
        spread = stem_spread(stem_ref, flat, base)
        for slot, block in uses:
            stem_w[slot] = stem_block(spread, base, BLOCKS[block])
    conv_w[...] = jnp.zeros_like(conv_w)
    for n, block in enumerate(BLOCKS):
        for d in range(3):
            for q, (_, side, tap) in enumerate(block):
                row = d * 256 + q * 64
                conv_w[n, row:row + 64, side * 128:side * 128 + 128] = conv_ref[d, tap]
    row, col = iota((192, 256), 0), iota((192, 256), 1)
    tap_row, g = row >> 4, row & 15
    a, d = tap_row & 3, tap_row >> 2
    row_of = 16 * g + 4 * (d - 1) + a
    good = (row_of == col) & ((d > 0) | ((g & 7) > 0))
    picked[...] = jnp.where(good, 1.0, 0.0).astype(BF16)


def encode_step(step, n_tiles, pix_ref, point_ref, stem_w, conv_w, picked, packed, hidden, middle, pooled):
    n_blocks = n_tiles // 2
    n_rows = n_tiles * 8
    for b in range(n_blocks):
        rows = dot(picked[...], pix_ref[b * 256:b * 256 + 256, :]).astype(BF16)
        for d in range(3):
            for pair in range(2):
                first = (d * 4 + pair * 2) * 16
                p0, p1 = rows[first:first + 16], rows[first + 16:first + 32]
                for c in range(3):
                    lo = c * 128
                    for half in range(2):
                        unit = 2 * c + half
                        at = lo + half * 64
                        h, u = unit // 3, unit % 3
                        packed[u, (h * 3 + d) * n_rows + b * 16:(h * 3 + d) * n_rows + b * 16 + 16,
                               pair * 128:pair * 128 + 128] = jnp.concatenate(
                                   [p0[:, at:at + 64], p1[:, at:at + 64]], axis=1)

    for n, terms in enumerate((((0, 0),), ((0, 1), (1, 2)), ((2, 3),))):
        total = dot(packed[terms[0][0]], stem_w[terms[0][1]])
        for u, w in terms[1:]:
            total = total + dot(packed[u], stem_w[w])
        total = jnp.maximum(total, 0.0).astype(BF16)
        for h in range(2):
            for d in range(3):
                hidden[n, h * n_rows:(h + 1) * n_rows, d * 256:(d + 1) * 256] = (
                    total[(h * 3 + d) * n_rows:(h * 3 + d + 1) * n_rows])
    left = dot(hidden[0], conv_w[0])
    mid = dot(hidden[1], conv_w[1])
    right = dot(hidden[2], conv_w[2])
    for h in range(2):
        rows = slice(h * n_rows, (h + 1) * n_rows)
        first = left[rows, :128]
        if h == 1:
            first = first + right[:n_rows, 128:]
        cols = (first, left[rows, 128:] + mid[rows, :128], mid[rows, 128:], right[rows, :128])
        for j, col in enumerate(cols):
            at = (h * 4 + j) * n_rows
            middle[at:at + n_rows, :] = jnp.maximum(col, 0.0).astype(BF16)
    point = jnp.maximum(dot(middle[...], point_ref[...]), 0.0)
    summed = point[:n_rows]
    for j in range(1, 8):
        summed = summed + point[j * n_rows:(j + 1) * n_rows]
    mean = jnp.sum(summed.reshape(n_tiles, 8, C3), axis=1) * (1.0 / 64.0)
    pooled[pl.ds(pl.multiple_of(step * n_tiles, n_tiles), n_tiles), :] = mean.astype(BF16)


def route(ids_ref, proj_ref, pooled, sent):
    embed = dot(pooled[...], proj_ref[...]).astype(BF16)
    n = embed.shape[0]
    across = jnp.broadcast_to(ids_ref[...], (n, n))
    own = iota((n, n), 0) == iota((n, n), 1)
    down = jnp.sum(jnp.where(own, across, 0), axis=1, keepdims=True)
    same = (down == across) & (iota((n, n), 0) < iota((n, n), 1))
    rank = jnp.sum(jnp.where(same, 1, 0), axis=0, keepdims=True)
    slot = ids_ref[...] * 8 + rank
    n_slots = sent.shape[0] * 8
    placed = jnp.where(iota((n_slots, n), 0) == slot, 1.0, 0.0)
    live = jnp.sum(placed, axis=1, keepdims=True)
    routed = dot(placed.astype(BF16), embed)
    sent[:, :, :D] = routed.reshape(n_slots // 8, 8, D).astype(BF16)
    sent[:, :, D:] = jnp.broadcast_to(live, (n_slots, 128)).reshape(n_slots // 8, 8, 128).astype(BF16)


def spread_rows(n, minor):
    row, col = iota((n, n), 0), iota((n, n), 1)
    shift = minor.bit_length() - 1
    return jnp.where(col == (row & (minor - 1)) * (n // minor) + (row >> shift), 1.0, 0.0).astype(BF16)


def dot_t(a, b):
    return lax.dot_general(a, b, (((1,), (1,)), ((), ())), preferred_element_type=F32)


def layer(t, s, n_tile, n_seq, sent, load_qkv, load_out, o_ref, got, qkv_w, out_w, kv_send, kv_all, context,
          send_sem, recv_sem, kv_send_sem, kv_recv_sem):
    moves = []
    for k in range(1, n_tile):
        peer = lax.rem(t + k, n_tile)
        moves.append(pltpu.make_async_remote_copy(
            src_ref=sent.at[peer], dst_ref=got.at[t], send_sem=send_sem.at[k - 1], recv_sem=recv_sem.at[k - 1],
            device_id={"tile": peer}, device_id_type=MESH))
        moves[-1].start()
    n = n_tile * 8
    low = iota((n, 128), 1) < HEAD_SIZE
    got[t] = sent[t]
    for move in moves:
        move.wait()

    natural = got[...].astype(F32).reshape(n, LINE)
    rows = dot(spread_rows(n, n_tile), natural.astype(BF16))
    live = rows[:, D:]
    rows = rows[:, :D]
    power = jnp.mean(rows * rows, axis=-1, keepdims=True)
    normed = (rows * lax.rsqrt(power + 1e-06)).astype(BF16)
    load_qkv.wait()
    pairs = D // 128
    kv = dot(normed, qkv_w[:, D:]).astype(BF16)
    low16 = low[:n_tile]

    def offsets(m):
        a = (2 * m) % n_seq
        b = (2 * m + 1) % n_seq
        return slice(a * n_tile, (a + 1) * n_tile), slice(b * n_tile, (b + 1) * n_tile)

    for m in range(2 * pairs):
        chunk = kv[:, m * 128:(m + 1) * 128]
        first, second = offsets(m % pairs)
        kv_send[m] = jnp.where(low16, chunk[first], chunk[second])
    flags = jnp.zeros((n_tile, 128), F32)
    for r in range(n_seq):
        flags = jnp.where(iota((n_tile, 128), 1) == r, live[r * n_tile:(r + 1) * n_tile], flags)
    kv_send[2 * pairs] = flags.astype(BF16)
    kv_moves = []
    for k in range(1, n_seq):
        peer = lax.rem(s + k, n_seq)
        kv_moves.append(pltpu.make_async_remote_copy(
            src_ref=kv_send, dst_ref=kv_all.at[s], send_sem=kv_send_sem.at[k - 1], recv_sem=kv_recv_sem.at[k - 1],
            device_id={"seq": peer}, device_id_type=MESH))
        kv_moves[-1].start()
    kv_all[s] = kv_send[...]

    query = (dot(normed, qkv_w[:, :D]).astype(BF16) * 0.125).astype(BF16)
    live_across = jnp.transpose(live)
    own = iota((n, n), 0) == iota((n, n), 1)
    bias = jnp.where((live_across > 0.5) | own, 0.0, -1e30)
    bias = jnp.concatenate([bias, bias], axis=0)
    none = jnp.zeros((n, 128), BF16)
    kept = []
    for m in range(pairs):
        lanes = slice(m * 128, (m + 1) * 128)
        q = query[:, lanes]
        q = jnp.concatenate([jnp.where(low, q, none), jnp.where(low, none, q)], axis=0)
        score = dot_t(q, kv[:, lanes]) + bias
        top = jnp.max(score, axis=-1, keepdims=True)
        weight = jnp.exp(score - top)
        total = jnp.sum(weight, axis=-1, keepdims=True)
        summed = dot(weight.astype(BF16), kv[:, D + m * 128:D + (m + 1) * 128])
        result = summed / total
        context[:, lanes] = jnp.where(low, result[:n], result[n:]).astype(BF16)
        first, second = offsets(m)
        second = slice(n + second.start, n + second.stop)
        kept.append([jnp.concatenate([x[first], x[second]], axis=0) for x in (q, top, total, summed)])

    for move in kv_moves:
        move.wait()
    there = kv_all[:, 2 * pairs].reshape(n, 128)
    pick = jnp.where(iota((n_tile, 128), 0) == iota((n_tile, 128), 1), 1.0, 0.0).astype(BF16)
    far_bias = jnp.where(dot_t(pick, there) > 0.5, 0.0, -1e30)
    for m in range(pairs):
        lanes = slice(m * 128, (m + 1) * 128)
        first, second = offsets(m)
        q, top, total, summed = kept[m]
        a, b = first.start // n_tile, second.start // n_tile
        far = jnp.concatenate([jnp.broadcast_to(far_bias[a:a + 1], (n_tile, 128)),
                               jnp.broadcast_to(far_bias[b:b + 1], (n_tile, 128))], axis=0)
        score = dot_t(q, kv_all[:, m].reshape(n, 128)) + far
        new_top = jnp.maximum(top, jnp.max(score, axis=-1, keepdims=True))
        weight = jnp.exp(score - new_top)
        scale = jnp.exp(top - new_top)
        total = total * scale + jnp.sum(weight, axis=-1, keepdims=True)
        summed = summed * scale + dot(weight.astype(BF16), kv_all[:, pairs + m].reshape(n, 128))
        result = (summed / total).astype(BF16)
        context[first, lanes] = jnp.where(low16, result[:n_tile], context[first, lanes])
        context[second, lanes] = jnp.where(low16, context[second, lanes], result[n_tile:])

    back = dot(spread_rows(n, n_seq), context[...]).astype(BF16)
    load_out.wait()
    final = dot(back, out_w[...])
    alive = natural[:, D:] > 0.5
    for m in range(pairs):
        lanes = slice(m * 128, (m + 1) * 128)
        o_ref[:, lanes] = jnp.where(alive, final[:, lanes], 0.0).astype(BF16)


def whole_kernel(steps, n_tile, n_seq, pix_ref, ids_ref, stem_ref, conv_ref, point_ref, proj_ref, qkv_hbm, out_hbm, o_ref,
                 flat, stem_w, conv_w, picked, packed, hidden, middle, pooled, sent,
                 got, qkv_w, out_w, kv_send, kv_all, context,
                 weight_sem, send_sem, recv_sem, kv_send_sem, kv_recv_sem):
    step = pl.program_id(0)
    n_tiles = pix_ref.shape[0] // 128
    t, s = lax.axis_index("tile"), lax.axis_index("seq")
    load_qkv = pltpu.make_async_copy(qkv_hbm, qkv_w, weight_sem.at[0])
    load_out = pltpu.make_async_copy(out_hbm, out_w, weight_sem.at[1])
    barrier = pltpu.get_barrier_semaphore()

    @pl.when(step == 0)
    def _():
        for k in range(1, n_tile):
            pl.semaphore_signal(barrier, inc=1, device_id={"tile": lax.rem(t + k, n_tile)}, device_id_type=MESH)
        for k in range(1, n_seq):
            pl.semaphore_signal(barrier, inc=1, device_id={"seq": lax.rem(s + k, n_seq)}, device_id_type=MESH)
        prepare(stem_ref, conv_ref, flat, stem_w, conv_w, picked)

    encode_step(step, n_tiles, pix_ref, point_ref, stem_w, conv_w, picked, packed, hidden, middle, pooled)

    @pl.when(step == steps - 1)
    def _():
        load_qkv.start()
        load_out.start()
        route(ids_ref, proj_ref, pooled, sent)
        pl.semaphore_wait(barrier, n_tile + n_seq - 2)
        layer(t, s, n_tile, n_seq, sent, load_qkv, load_out, o_ref, got, qkv_w, out_w, kv_send, kv_all, context,
              send_sem, recv_sem, kv_send_sem, kv_recv_sem)


def body(
    pixels, encoder_ids, stem_weight, conv_weight, point_weight, proj_weight, qkv_weight, out_weight
):
    n_tile, n_seq = lax.axis_size("tile"), lax.axis_size("seq")
    steps = 4
    tiles = pixels.shape[0]
    rows = tiles * 128 // steps
    n_rows = rows // 16
    n = n_tile * 8
    blocks = 2 * D // 128 + 1
    stem_t = jnp.transpose(stem_weight, (0, 2, 1, 3))
    whole = lambda shape: pl.BlockSpec(shape, lambda i: (0,) * len(shape))
    anywhere = pl.BlockSpec(memory_space=pl.ANY)
    out = pl.pallas_call(
        functools.partial(whole_kernel, steps, n_tile, n_seq),
        grid=(steps,),
        in_specs=[
            pl.BlockSpec((rows, 384), lambda i: (i, 0)),
            whole((1, tiles)),
            whole(stem_t.shape),
            whole(conv_weight.shape),
            whole(point_weight.shape),
            whole(proj_weight.shape),
            anywhere,
            anywhere,
        ],
        out_specs=whole((n, D)),
        out_shape=jax.ShapeDtypeStruct((n, D), BF16),
        scratch_shapes=[
            pltpu.VMEM((64, 64), F32),
            pltpu.VMEM((4, 256, 256), BF16),
            pltpu.VMEM((3, 768, 256), BF16),
            pltpu.VMEM((192, 256), BF16),
            pltpu.VMEM((3, 6 * n_rows, 256), BF16),
            pltpu.VMEM((3, 2 * n_rows, 768), BF16),
            pltpu.VMEM((8 * n_rows, 128), BF16),
            pltpu.VMEM((tiles, C3), BF16),
            pltpu.VMEM((n_tile, 8, LINE), BF16),
            pltpu.VMEM((n_tile, 8, LINE), BF16),
            pltpu.VMEM(qkv_weight.shape, BF16),
            pltpu.VMEM(out_weight.shape, BF16),
            pltpu.VMEM((blocks, n_tile, 128), BF16),
            pltpu.VMEM((n_seq, blocks, n_tile, 128), BF16),
            pltpu.VMEM((n, D), BF16),
            pltpu.SemaphoreType.DMA((2,)),
            pltpu.SemaphoreType.DMA((n_tile - 1,)),
            pltpu.SemaphoreType.DMA((n_tile - 1,)),
            pltpu.SemaphoreType.DMA((n_seq - 1,)),
            pltpu.SemaphoreType.DMA((n_seq - 1,)),
        ],
        compiler_params=pltpu.CompilerParams(collective_id=0, has_side_effects=True),
        name="tiles_to_slide",
    )(pixels.reshape(tiles * 128, 384), encoder_ids.reshape(1, tiles), stem_t, conv_weight, point_weight, proj_weight,
      qkv_weight, out_weight)
    return out[None]


def solution(mesh):
    return jax.shard_map(
        body,
        mesh=mesh,
        in_specs=(
            P(("tile", "seq"), None, None),
            P(("tile", "seq"), None),
            P(),
            P(),
            P(),
            P(),
            P(),
            P(),
        ),
        out_specs=P("tile", "seq", None),
        check_vma=False,
    )
```

```python
import functools
import math
import jax
import jax.numpy as jnp
from jax import lax
from jax.sharding import PartitionSpec as P
from jax.experimental import pallas as pl
from jax.experimental.pallas import tpu as pltpu

D = 768
C1, C2, C3 = 64, 128, 256
GROUP = 16
LINE = D + 128
HEAD_SIZE = 64
F32, BF16 = jnp.float32, jnp.bfloat16
MESH = pl.DeviceIdType.MESH

BLOCKS = (
    ((0, 0, 1), (1, 0, 2), (3, 1, 0), (4, 1, 1)),
    ((5, 0, 2), (7, 1, 0), (8, 1, 1), (9, 1, 2)),
    ((11, 0, 0), (12, 0, 1), (13, 0, 2), (15, 1, 0)),
)


def iota(shape, dim):
    return lax.broadcasted_iota(jnp.int32, shape, dim)


def dot(a, b):
    return jnp.dot(a, b, preferred_element_type=F32)


def stem_spread(flat_ref, base):
    taps = iota((64, 64), 1)
    lane = iota((64, 64), 0) + base
    lane = lane - 12 * jnp.floor((lane.astype(F32) + 0.5) * (1.0 / 12.0)).astype(jnp.int32)
    colour, column = (taps & 15) >> 2, taps & 3
    hit = jnp.where((colour < 3) & (lane == 3 * column + colour), 1.0, 0.0)
    chosen = jnp.concatenate([jnp.where((taps >> 4) == a, hit, 0.0) for a in range(4)], axis=0)
    tiled = jnp.where((iota((64, 256), 1) & 63) == iota((64, 256), 0), 1.0, 0.0).astype(BF16)
    wide = dot(flat_ref[...].astype(BF16), tiled).astype(BF16)
    return dot(chosen.astype(BF16), wide)


def stem_block(spread, base, block):
    quarter = iota((1, 256), 1) >> 6
    first = jnp.zeros((1, 256), jnp.int32)
    for q, (column, _, _) in enumerate(block):
        first = jnp.where(quarter == q, 12 * column, first)
    lane = iota((64, 256), 0) + base - first
    inside = (lane >= 0) & (lane < 12)
    return jnp.concatenate([jnp.where(inside, spread[a * 64:(a + 1) * 64], 0.0) for a in range(4)], axis=0).astype(BF16)


def prepare(stem_ref, conv_ref, flat, stem_w, conv_w, picked):
    flat[...] = jnp.zeros_like(flat)
    for a in range(4):
        for c in range(3):
            flat[a * 16 + c * 4:a * 16 + c * 4 + 4, :] = stem_ref[a, c].astype(F32)
    for base, uses in ((0, ((0, 0), (1, 1))), (64, ((2, 1),)), (128, ((3, 2),))):
        spread = stem_spread(flat, base)
        for slot, block in uses:
            stem_w[slot] = stem_block(spread, base, BLOCKS[block])
    none = jnp.zeros((64, 128), BF16)
    for n, block in enumerate(BLOCKS):
        for d in range(3):
            for q, (_, side, tap) in enumerate(block):
                row = d * 256 + q * 64
                conv_w[n, row:row + 64, side * 128:side * 128 + 128] = conv_ref[d, tap]
                conv_w[n, row:row + 64, (1 - side) * 128:(1 - side) * 128 + 128] = none
    row, col = iota((192, 256), 0), iota((192, 256), 1)
    tap_row, g = row >> 4, row & 15
    a, d = tap_row & 3, tap_row >> 2
    row_of = 16 * g + 4 * (d - 1) + a
    good = (row_of == col) & ((d > 0) | ((g & 7) > 0))
    picked[...] = jnp.where(good, 1.0, 0.0).astype(BF16)


def regroup(first_row, n_tiles, pix, picked, packed):
    n_blocks, n_rows = n_tiles // 2, n_tiles * 8
    low = iota((16, 128), 1) < 64
    for b in range(n_blocks):
        rows = dot(picked[...], pix[first_row + b * 256:first_row + b * 256 + 256, :])
        for d in range(3):
            for pair in range(2):
                first = (d * 4 + pair * 2) * 16
                for c in range(3):
                    lanes = slice(c * 128, (c + 1) * 128)
                    p0, p1 = rows[first:first + 16, lanes], rows[first + 16:first + 32, lanes]
                    r0, r1 = pltpu.roll(p0, 64, 1), pltpu.roll(p1, 64, 1)
                    for half, both in enumerate((jnp.where(low, p0, r1), jnp.where(low, r0, p1))):
                        h, u = divmod(2 * c + half, 3)
                        at = (h * 3 + d) * n_rows + b * 16
                        packed[u, at:at + 16, pair * 128:pair * 128 + 128] = both.astype(BF16)


def convolve(chunk, n_tiles, point_ref, stem_w, conv_w, packed, hidden, middle, pooled):
    n_rows = n_tiles * 8
    for n, terms in enumerate((((0, 0),), ((0, 1), (1, 2)), ((2, 3),))):
        total = dot(packed[terms[0][0]], stem_w[terms[0][1]])
        for u, w in terms[1:]:
            total = total + dot(packed[u], stem_w[w])
        total = jnp.maximum(total, 0.0).astype(BF16)
        for h in range(2):
            for d in range(3):
                hidden[n, h * n_rows:(h + 1) * n_rows, d * 256:(d + 1) * 256] = (
                    total[(h * 3 + d) * n_rows:(h * 3 + d + 1) * n_rows])
    left = dot(hidden[0], conv_w[0])
    mid = dot(hidden[1], conv_w[1])
    right = dot(hidden[2], conv_w[2])
    for h in range(2):
        rows = slice(h * n_rows, (h + 1) * n_rows)
        first = left[rows, :128]
        if h == 1:
            first = first + right[:n_rows, 128:]
        cols = (first, left[rows, 128:] + mid[rows, :128], mid[rows, 128:], right[rows, :128])
        for j, col in enumerate(cols):
            at = (h * 4 + j) * n_rows
            middle[at:at + n_rows, :] = jnp.maximum(col, 0.0).astype(BF16)
    point = jnp.maximum(dot(middle[...], point_ref[...]), 0.0)
    summed = point[:n_rows]
    for j in range(1, 8):
        summed = summed + point[j * n_rows:(j + 1) * n_rows]
    mean = jnp.sum(summed.reshape(n_tiles, 8, C3), axis=1) * (1.0 / 64.0)
    pooled[chunk * n_tiles:(chunk + 1) * n_tiles, :] = mean.astype(BF16)


def route(ids_ref, proj_ref, pooled, sent):
    embed = dot(pooled[...], proj_ref[...]).astype(BF16)
    n = embed.shape[0]
    across = jnp.broadcast_to(ids_ref[...], (n, n))
    own = iota((n, n), 0) == iota((n, n), 1)
    down = jnp.sum(jnp.where(own, across, 0), axis=1, keepdims=True)
    same = (down == across) & (iota((n, n), 0) < iota((n, n), 1))
    rank = jnp.sum(jnp.where(same, 1, 0), axis=0, keepdims=True)
    slot = ids_ref[...] * 8 + rank
    n_slots = sent.shape[0] * 8
    placed = jnp.where(iota((n_slots, n), 0) == slot, 1.0, 0.0)
    live = jnp.sum(placed, axis=1, keepdims=True)
    routed = dot(placed.astype(BF16), embed)
    sent[:, :, :D] = routed.reshape(n_slots // 8, 8, D).astype(BF16)
    sent[:, :, D:] = jnp.broadcast_to(live, (n_slots, 128)).reshape(n_slots // 8, 8, 128).astype(BF16)


def spread_rows(n, minor):
    row, col = iota((n, n), 0), iota((n, n), 1)
    shift = minor.bit_length() - 1
    return jnp.where(col == (row & (minor - 1)) * (n // minor) + (row >> shift), 1.0, 0.0).astype(BF16)


def dot_t(a, b):
    return lax.dot_general(a, b, (((1,), (1,)), ((), ())), preferred_element_type=F32)


def torus_order(n):
    side = math.isqrt(n)
    hops = lambda k: sum(min(d, side - d) for d in divmod(k, side))
    return sorted(range(1, n), key=lambda k: (-hops(k), k))


def torus_peer(t, k, n):
    side = math.isqrt(n)
    return lax.rem(t // side + k // side, side) * side + lax.rem(lax.rem(t, side) + k % side, side)


def layer(t, s, n_tile, n_seq, sent, load_qkv, load_out, o_ref, got, qkv_w, out_w, kv_send, kv_all, context,
          send_sem, recv_sem, kv_send_sem, kv_recv_sem):
    moves = []
    for k in torus_order(n_tile):
        peer = torus_peer(t, k, n_tile)
        moves.append(pltpu.make_async_remote_copy(
            src_ref=sent.at[peer], dst_ref=got.at[t], send_sem=send_sem.at[k - 1], recv_sem=recv_sem.at[k - 1],
            device_id={"tile": peer}, device_id_type=MESH))
        moves[-1].start()
    n = n_tile * 8
    low = iota((n, 128), 1) < HEAD_SIZE
    got[t] = sent[t]
    for move in moves:
        move.wait()

    natural = got[...].astype(F32).reshape(n, LINE)
    rows = dot(spread_rows(n, n_tile), natural.astype(BF16))
    live = rows[:, D:]
    rows = rows[:, :D]
    power = jnp.mean(rows * rows, axis=-1, keepdims=True)
    normed = (rows * lax.rsqrt(power + 1e-06)).astype(BF16)
    load_qkv.wait()
    pairs = D // 128
    kv = dot(normed, qkv_w[:, D:]).astype(BF16)
    low16 = low[:n_tile]

    def offsets(m):
        a = (2 * m) % n_seq
        b = (2 * m + 1) % n_seq
        return slice(a * n_tile, (a + 1) * n_tile), slice(b * n_tile, (b + 1) * n_tile)

    for m in range(2 * pairs):
        chunk = kv[:, m * 128:(m + 1) * 128]
        first, second = offsets(m % pairs)
        kv_send[m] = jnp.where(low16, chunk[first], chunk[second])
    flags = jnp.zeros((n_tile, 128), F32)
    for r in range(n_seq):
        flags = jnp.where(iota((n_tile, 128), 1) == r, live[r * n_tile:(r + 1) * n_tile], flags)
    kv_send[2 * pairs] = flags.astype(BF16)
    twin = s + 1 - 2 * lax.rem(s, 2)
    far_offsets = sorted(range(2, n_seq, 2), key=lambda k: (-min(k, n_seq - k), k))
    kv_moves, forwards = {}, {}
    for k in far_offsets:
        kv_moves[k] = pltpu.make_async_remote_copy(
            src_ref=kv_send, dst_ref=kv_all.at[s], send_sem=kv_send_sem.at[k - 1], recv_sem=kv_recv_sem.at[k - 1],
            device_id={"seq": lax.rem(s + k, n_seq)}, device_id_type=MESH)
        kv_moves[k].start()
    to_twin = pltpu.make_async_remote_copy(
        src_ref=kv_send, dst_ref=kv_all.at[s], send_sem=kv_send_sem.at[0], recv_sem=kv_recv_sem.at[0],
        device_id={"seq": twin}, device_id_type=MESH)
    to_twin.start()
    kv_all[s] = kv_send[...]

    def hand_on(k):
        kv_moves[k].wait_recv()
        source = lax.rem(s + n_seq - k, n_seq)
        forwards[k] = pltpu.make_async_remote_copy(
            src_ref=kv_all.at[source], dst_ref=kv_all.at[source], send_sem=kv_send_sem.at[k], recv_sem=kv_recv_sem.at[k],
            device_id={"seq": twin}, device_id_type=MESH)
        forwards[k].start()

    query = (dot(normed, qkv_w[:, :D]).astype(BF16) * 0.125).astype(BF16)
    live_across = jnp.transpose(live)
    own = iota((n, n), 0) == iota((n, n), 1)
    bias = jnp.where((live_across > 0.5) | own, 0.0, -1e30)
    bias = jnp.concatenate([bias, bias], axis=0)
    none = jnp.zeros((n, 128), BF16)
    kept = []
    for m in range(pairs):
        lanes = slice(m * 128, (m + 1) * 128)
        q = query[:, lanes]
        q = jnp.concatenate([jnp.where(low, q, none), jnp.where(low, none, q)], axis=0)
        score = dot_t(q, kv[:, lanes]) + bias
        top = jnp.max(score, axis=-1, keepdims=True)
        weight = jnp.exp(score - top)
        total = jnp.sum(weight, axis=-1, keepdims=True)
        summed = dot(weight.astype(BF16), kv[:, D + m * 128:D + (m + 1) * 128])
        result = summed / total
        context[:, lanes] = jnp.where(low, result[:n], result[n:]).astype(BF16)
        first, second = offsets(m)
        second = slice(n + second.start, n + second.stop)
        if m == pairs - 3:
            for k in far_offsets[1:]:
                hand_on(k)
        kept.append([jnp.concatenate([x[first], x[second]], axis=0) for x in (q, top, total, summed)])

    hand_on(far_offsets[0])
    to_twin.wait()
    for k in far_offsets:
        kv_moves[k].wait_send()
    for k in far_offsets:
        forwards[k].wait()
    there = kv_all[:, 2 * pairs].reshape(n, 128)
    pick = jnp.where(iota((n_tile, 128), 0) == iota((n_tile, 128), 1), 1.0, 0.0).astype(BF16)
    far_bias = jnp.where(dot_t(pick, there) > 0.5, 0.0, -1e30)
    scores = []
    for m in range(pairs):
        for half in offsets(m):
            a = half.start // n_tile
            scores.append(jnp.broadcast_to(far_bias[a:a + 1], (n_tile, 128)))
    join = lambda parts: jnp.concatenate(parts, axis=0)
    q, top, total, summed = [join(parts) for parts in zip(*kept)]
    size = 2 * n_tile
    block = lambda x, m: x[m * size:(m + 1) * size]
    score = join([dot_t(block(q, m), kv_all[:, m].reshape(n, 128)) for m in range(pairs)]) + join(scores)
    new_top = jnp.maximum(top, jnp.max(score, axis=-1, keepdims=True))
    weight = jnp.exp(score - new_top)
    scale = jnp.exp(top - new_top)
    total = total * scale + jnp.sum(weight, axis=-1, keepdims=True)
    weight = weight.astype(BF16)
    more = join([dot(block(weight, m), kv_all[:, pairs + m].reshape(n, 128)) for m in range(pairs)])
    result = ((summed * scale + more) / total).astype(BF16)
    for m in range(pairs):
        lanes = slice(m * 128, (m + 1) * 128)
        first, second = offsets(m)
        mine = block(result, m)
        context[first, lanes] = jnp.where(low16, mine[:n_tile], context[first, lanes])
        context[second, lanes] = jnp.where(low16, context[second, lanes], mine[n_tile:])

    back = dot(spread_rows(n, n_seq), context[...]).astype(BF16)
    load_out.wait()
    final = dot(back, out_w[...])
    alive = natural[:, D:] > 0.5
    for m in range(pairs):
        lanes = slice(m * 128, (m + 1) * 128)
        o_ref[:, lanes] = jnp.where(alive, final[:, lanes], 0.0).astype(BF16)


def whole_kernel(chunks, n_tile, n_seq, pix_hbm, ids_hbm, stem_hbm, conv_hbm, point_hbm, proj_hbm, qkv_hbm, out_hbm, o_ref,
                 pix, ids, stem, conv, point, proj, qkv_w, out_w,
                 flat, stem_w, conv_w, picked, packed_a, packed_b, hidden, middle, pooled, sent,
                 got, kv_send, kv_all, context,
                 pix_sem, weight_sem, send_sem, recv_sem, kv_send_sem, kv_recv_sem):
    rows = pix.shape[0] // chunks
    n_tiles = rows // 128
    t, s = lax.axis_index("tile"), lax.axis_index("seq")
    part = lambda ref, i: ref.at[pl.ds(i * rows, rows)]
    load_pix = [pltpu.make_async_copy(part(pix_hbm, i), part(pix, i), pix_sem.at[i]) for i in range(chunks)]
    pairs = ((stem_hbm, stem), (conv_hbm, conv), (point_hbm, point), (ids_hbm, ids), (proj_hbm, proj),
             (qkv_hbm, qkv_w), (out_hbm, out_w))
    load_stem, load_conv, load_point, load_ids, load_proj, load_qkv, load_out = [
        pltpu.make_async_copy(a, b, weight_sem.at[i]) for i, (a, b) in enumerate(pairs)]
    for load in (load_stem, load_conv, load_pix[0], load_point, *load_pix[1:], load_ids, load_proj, load_qkv, load_out):
        load.start()
    barrier = pltpu.get_barrier_semaphore()
    for k in range(1, n_tile):
        pl.semaphore_signal(barrier, inc=1, device_id={"tile": lax.rem(t + k, n_tile)}, device_id_type=MESH)
    for k in range(1, n_seq):
        pl.semaphore_signal(barrier, inc=1, device_id={"seq": lax.rem(s + k, n_seq)}, device_id_type=MESH)
    load_stem.wait()
    load_conv.wait()
    prepare(stem, conv, flat, stem_w, conv_w, picked)
    packed = (packed_a, packed_b)
    for i in range(chunks + 1):
        if i < chunks:
            load_pix[i].wait()
            if i == 0:
                load_point.wait()
            regroup(i * rows, n_tiles, pix, picked, packed[i % 2])
        if i > 0:
            convolve(i - 1, n_tiles, point, stem_w, conv_w, packed[(i - 1) % 2], hidden, middle, pooled)
    load_ids.wait()
    load_proj.wait()
    route(ids, proj, pooled, sent)
    pl.semaphore_wait(barrier, n_tile + n_seq - 2)
    layer(t, s, n_tile, n_seq, sent, load_qkv, load_out, o_ref, got, qkv_w, out_w, kv_send, kv_all, context,
          send_sem, recv_sem, kv_send_sem, kv_recv_sem)


def body(
    pixels, encoder_ids, stem_weight, conv_weight, point_weight, proj_weight, qkv_weight, out_weight
):
    n_tile, n_seq = lax.axis_size("tile"), lax.axis_size("seq")
    chunks = 4
    tiles = pixels.shape[0]
    n_rows = tiles // chunks * 8
    n = n_tile * 8
    blocks = 2 * D // 128 + 1
    operands = (pixels.reshape(tiles * 128, 384), encoder_ids.reshape(1, tiles), jnp.transpose(stem_weight, (0, 2, 1, 3)),
                conv_weight, point_weight, proj_weight, qkv_weight, out_weight)
    out = pl.pallas_call(
        functools.partial(whole_kernel, chunks, n_tile, n_seq),
        in_specs=[pl.BlockSpec(memory_space=pl.ANY)] * len(operands),
        out_specs=pl.BlockSpec(memory_space=pltpu.VMEM),
        out_shape=jax.ShapeDtypeStruct((n, D), BF16),
        scratch_shapes=[pltpu.VMEM(x.shape, x.dtype) for x in operands] + [
            pltpu.VMEM((64, 64), F32),
            pltpu.VMEM((4, 256, 256), BF16),
            pltpu.VMEM((3, 768, 256), BF16),
            pltpu.VMEM((192, 256), BF16),
            pltpu.VMEM((3, 6 * n_rows, 256), BF16),
            pltpu.VMEM((3, 6 * n_rows, 256), BF16),
            pltpu.VMEM((3, 2 * n_rows, 768), BF16),
            pltpu.VMEM((8 * n_rows, 128), BF16),
            pltpu.VMEM((tiles, C3), BF16),
            pltpu.VMEM((n_tile, 8, LINE), BF16),
            pltpu.VMEM((n_tile, 8, LINE), BF16),
            pltpu.VMEM((blocks, n_tile, 128), BF16),
            pltpu.VMEM((n_seq, blocks, n_tile, 128), BF16),
            pltpu.VMEM((n, D), BF16),
            pltpu.SemaphoreType.DMA((chunks,)),
            pltpu.SemaphoreType.DMA((len(operands) - 1,)),
            pltpu.SemaphoreType.DMA((n_tile - 1,)),
            pltpu.SemaphoreType.DMA((n_tile - 1,)),
            pltpu.SemaphoreType.DMA((n_seq - 1,)),
            pltpu.SemaphoreType.DMA((n_seq - 1,)),
        ],
        compiler_params=pltpu.CompilerParams(collective_id=0, has_side_effects=True),
        name="tiles_to_slide",
    )(*operands)
    return out[None]


def solution(mesh):
    return jax.shard_map(
        body,
        mesh=mesh,
        in_specs=(
            P(("tile", "seq"), None, None),
            P(("tile", "seq"), None),
            P(),
            P(),
            P(),
            P(),
            P(),
            P(),
        ),
        out_specs=P("tile", "seq", None),
        check_vma=False,
    )
```
